128 devices in a mesh: ka: 64 (over y, z_lo, x, core), br: 2 (over z_hi).
Axes of the slice: x: 4, y: 4, z: 4 (z_hi: 2, z_lo: 2; z = z_hi * 2 + z_lo), core: 2. Of those that a mesh axis runs over, the one named last changes fastest.
Arguments:
- occupation: float32 [8, 32768], P(None, 'ka'), may hold values from 0 to 1
- phonons: float32 [12, 4096], P('br', 'ka'), may hold values from 0.05 to 5
- coupling: bfloat16 [16, 12, 8, 8, 32768], P(None, 'br', None, None, 'ka'), may hold values from 0.00049972534 to 0.0079956055
- shifted_point_index: int32 [16, 32768], P(None, 'ka'), may hold values from 0 to 32767
- wavevector_index: int32 [16, 32768], P(None, 'ka'), may hold values from 0 to 4095
- window: int32 [8, 32768], P(None, 'ka'), may hold values 0 or 1
Outputs:
- collision: float32 [8, 32768], P(None, 'ka')
- generation: float32 [12, 4096], P('br', 'ka')
The draws below stay inside these ranges and needn't reach their ends.
All inputs are finite; a program needn't handle non-finite values. No bound on the sum of `window` on one device may be relied on, other than what follows from the above.
Results may differ from the reference program's by a relative error of at most 0.0003.
Values sent between devices are 32-bit elements; how exact they have to be, the bound alone decides.
No kernel may reach another device: no remote copies, remote signals or barrier semaphores. Data moves between devices by JAX's collectives and lax.ppermute only.
A program may use at most 128 MiB of HBM per device.

```python
import math
import jax
import jax.numpy as jnp
from jax import lax

NB = 8
NBR = 12
QSUB = 4096
QPK = 16
NK = 32768


def with_ends(values, stream_key, smallest, high):
    dims = values.shape
    spot = [jax.random.randint(jax.random.fold_in(stream_key, axis), (), 0, dims[axis]) for axis in range(len(dims))]
    values = values.at[tuple(spot)].set(smallest)
    longest = dims.index(max(dims))
    spot[longest] = (spot[longest] + 1) % dims[longest]
    return values.at[tuple(spot)].set(high)


def level_of(stream_key, shape, pieces, low, high):
    def one(position, blocks):
        steps = jax.random.uniform(jax.random.fold_in(jax.random.fold_in(stream_key, 6), position), (blocks,), jnp.float32, low / len(pieces), high / len(pieces))
        return jnp.repeat(jnp.exp(steps), shape[position] // blocks).reshape((-1,) + (1,) * (len(shape) - position - 1))

    loudness = one(*pieces[0])
    for cut in pieces[1:]:
        loudness = loudness * one(*cut)
    return loudness


def setup_inputs(seed: int = 0) -> dict:
    keys = jax.random.split(jax.random.key(seed), 7)
    return {
        "occupation": jnp.clip(1.0 * jax.random.uniform(keys[0], (NB, NK), jnp.float32) ** level_of(keys[0], (NB, NK), ((1, 64),), -0.2, 0.2), 0.0, 1.0),
        "phonons": jnp.clip(jnp.exp(math.log(5.0) - 4.6051702 * jax.random.uniform(keys[1], (NBR, QSUB), jnp.float32) ** level_of(keys[1], (NBR, QSUB), ((0, 2), (1, 64)), -0.2, 0.2)), 0.05, 5.0),
        "coupling": jnp.clip(jnp.exp(math.log(0.0079956055) - 2.7725887 * jax.random.uniform(keys[2], (QPK, NBR, NB, NB, NK), jnp.float32) ** level_of(keys[2], (QPK, NBR, NB, NB, NK), ((1, 2), (4, 64)), -0.2, 0.2)), 0.00049972534, 0.0079956055).astype(jnp.bfloat16),
        "shifted_point_index": with_ends(jax.random.randint(keys[3], (QPK, NK), 0, NK), jax.random.fold_in(keys[3], 1), 0, NK - 1).astype(jnp.int32),
        "wavevector_index": with_ends(jax.random.randint(keys[4], (QPK, NK), 0, QSUB), jax.random.fold_in(keys[4], 1), 0, QSUB - 1).astype(jnp.int32),
        "window": with_ends((jax.random.randint(keys[5], (NB, NK), 0, 4) < 3).astype(jnp.int32), jax.random.fold_in(keys[5], 1), 0, 1),
    }


def apply_scattering(occupation, phonons, coupling, shifted_point_index, wavevector_index, window):
    window_f = window.astype(jnp.float32)

    def slot_step(loop_state, inputs):
        scattering_sum, emission_sum = loop_state
        tile, k_plus, q_rows = inputs
        tile = tile.astype(jnp.float32)
        beyond = occupation[:, k_plus]
        phonon_at = phonons[:, q_rows]
        weighted = jnp.einsum("umnk,nk->umk", tile, beyond)
        totals = jnp.sum(tile, axis=2)
        detailed_balance_term = window_f[None] * (weighted * (phonon_at[:, None, :] + 1.0) - occupation[None] * weighted - occupation[None] * totals * phonon_at[:, None, :])
        per_point = jnp.sum(detailed_balance_term, axis=1)
        collected_values = jax.ops.segment_sum(per_point.T, q_rows, num_segments=QSUB).T
        return (scattering_sum + jnp.sum(detailed_balance_term, axis=0), emission_sum + collected_values), None

    start = (jnp.zeros(occupation.shape, jnp.float32), jnp.zeros(phonons.shape, jnp.float32))
    result, _ = lax.scan(slot_step, start, (coupling, shifted_point_index, wavevector_index))
    return result[0], result[1] / 16.0


def reference(occupation, phonons, coupling, shifted_point_index, wavevector_index, window):
    initial_scattering, initial_emission = apply_scattering(occupation, phonons, coupling, shifted_point_index, wavevector_index, window)
    halfway_occupancy = occupation + 0.1 * initial_scattering
    mid_phonons = phonons + 0.1 * initial_emission
    collision, generation = apply_scattering(halfway_occupancy, mid_phonons, coupling, shifted_point_index, wavevector_index, window)
    return collision, generation
```

```python
import functools
import jax
import jax.numpy as jnp
from jax import lax
from jax.experimental import pallas as pl
from jax.experimental.pallas import tpu as pltpu
from jax.sharding import Mesh, PartitionSpec as P

F32 = jnp.float32
BF16 = jnp.bfloat16
CHIPS = ("y", "zl", "x")


def split2(a):
    hi = a.astype(BF16)
    return hi, (a - hi.astype(F32)).astype(BF16)


def phase_kernel(
    merge, par_ref, own_ref, oth_ref, f_ref, win_ref, idx_ref, q_ref, g_ref,
    c_ref, gen_ref, t2, p2, x, y, e_s, w_s, v_s, cacc, gacc,
):
    par = par_ref[0]
    for side, ref in enumerate((own_ref, oth_ref)):
        for b in range(2):
            for h in range(2):
                hi, lo = split2(ref[:, (2 * b + h) * 8 : (2 * b + h + 1) * 8, :])
                for part, val in enumerate((hi, lo)):
                    t2[side, :, b, :, part * 256 + h * 128 : part * 256 + (h + 1) * 128] = val
    ph = own_ref[:, 32:40, :]
    if merge:
        ph = ph + oth_ref[:, 32:40, :]
    ph = ph.reshape(16, 2, 8, 128)
    for h in range(2):
        hi, lo = split2(ph[:, h])
        p2[:, :, h * 128 : (h + 1) * 128] = hi
        p2[:, :, 256 + h * 128 : 256 + (h + 1) * 128] = lo
    cacc[...] = jnp.zeros_like(cacc)
    gacc[...] = jnp.zeros_like(gacc)
    t2m = t2.reshape(1024, 512)
    p2m = p2.reshape(128, 512)

    def slot(s, _):
        row = idx_ref[pl.ds(s, 1), :]
        qrow = q_ref[pl.ds(s, 1), :]
        io = lax.broadcasted_iota(jnp.int32, (256, 512), 0)
        oh = jnp.where(io == (row & 255), 1.0, 0.0).astype(BF16)
        ohq = jnp.where(io == (qrow & 255), 1.0, 0.0).astype(BF16)
        x[...] = jnp.dot(t2m[...], jnp.concatenate([oh, oh], axis=0), preferred_element_type=F32)
        y[...] = jnp.dot(p2m[...], jnp.concatenate([ohq, ohq], axis=0), preferred_element_type=F32)
        h = row >> 8
        h = (((h >> 1) & 1) ^ par) * 64 + (h >> 2) * 2 + (h & 1)
        h = jnp.broadcast_to(h, (8, 512))
        acc = [jnp.zeros((8, 512), F32) for _ in range(2)]
        for r in range(128):
            acc[r % 2] = jnp.where(h == r, x[r * 8 : (r + 1) * 8, :], acc[r % 2])
        e_s[...] = acc[0] + acc[1]
        hq = jnp.broadcast_to(qrow >> 8, (8, 512))
        acc = jnp.zeros((8, 512), F32)
        for r in range(16):
            acc = jnp.where(hq == r, y[r * 8 : (r + 1) * 8, :], acc)
        w_s[...] = acc
        for kb in range(4):
            cols = slice(kb * 128, (kb + 1) * 128)
            e = e_s[:, cols]
            d1, d2, ca = [], [], []
            for m in range(8):
                fm = f_ref[m : m + 1, cols]
                wm = win_ref[m : m + 1, cols].astype(F32)
                d1.append((wm * (1.0 - fm)) * e)
                d2.append(wm * (e - fm))
                ca.append(cacc[m, :, cols])
            for u in range(6):
                wu = jnp.broadcast_to(w_s[u : u + 1, cols], (8, 128))
                ga = None
                for m in range(8):
                    tm = g_ref[s, u, m, :, cols].astype(F32) * (d1[m] + wu * d2[m])
                    ca[m] = ca[m] + tm
                    ga = tm if ga is None else ga + tm
                v_s[u : u + 1, cols] = jnp.sum(ga, axis=0, keepdims=True)
            for m in range(8):
                cacc[m, :, cols] = ca[m]
        v = v_s[...]
        v1 = v.astype(BF16).astype(F32)
        r1 = v - v1
        v2 = r1.astype(BF16).astype(F32)
        v3 = r1 - v2
        hm = (lax.broadcasted_iota(jnp.int32, (16, 8, 512), 0)) == (qrow >> 8)[None]
        a = [
            jnp.where(hm, jnp.broadcast_to(vv[None], (16, 8, 512)), 0.0).astype(BF16).reshape(128, 512)
            for vv in (v1, v2, v3)
        ]
        gacc[...] += lax.dot_general(
            jnp.concatenate(a, axis=0), ohq, (((1,), (1,)), ((), ())), preferred_element_type=F32
        )
        return 0

    v_s[...] = jnp.zeros_like(v_s)
    lax.fori_loop(0, 16, slot, 0)
    for m in range(8):
        c_ref[m : m + 1, :] = jnp.sum(cacc[m], axis=0, keepdims=True)
    gs = (gacc[0:128] + gacc[128:256] + gacc[256:384]).reshape(16, 8, 256)
    for h in range(2):
        gen_ref[:, h] = gs[:, :, h * 128 : (h + 1) * 128]


def phase(merge, par, own, oth, f, win, idx, q, g):
    vm = pl.BlockSpec(memory_space=pltpu.VMEM)
    c, gen = pl.pallas_call(
        functools.partial(phase_kernel, merge),
        out_shape=(jax.ShapeDtypeStruct((8, 512), F32), jax.ShapeDtypeStruct((16, 2, 8, 128), F32)),
        in_specs=[pl.BlockSpec(memory_space=pltpu.SMEM)] + [vm] * 7,
        out_specs=(vm, vm),
        scratch_shapes=[
            pltpu.VMEM((2, 32, 2, 8, 512), BF16),
            pltpu.VMEM((16, 8, 512), BF16),
            pltpu.VMEM((1024, 512), F32),
            pltpu.VMEM((128, 512), F32),
            pltpu.VMEM((8, 512), F32),
            pltpu.VMEM((8, 512), F32),
            pltpu.VMEM((8, 512), F32),
            pltpu.VMEM((8, 8, 512), F32),
            pltpu.VMEM((384, 256), F32),
        ],
        name="phase",
    )(par, own, oth, f, win, idx, q, g)
    return c, gen.reshape(32, 8, 128)


def tiles(f):
    return f.reshape(8, 4, 128).transpose(1, 0, 2).reshape(32, 128)


def gather_all(chunk):
    send = jnp.broadcast_to(chunk[None], (32, 40, 128))
    own = lax.all_to_all(send, CHIPS, 0, 0, tiled=True)
    oth = lax.ppermute(own, "c", [(0, 1), (1, 0)])
    return own, oth


def on_device(f, p, g, idx, q, win):
    par = lax.axis_index("c").astype(jnp.int32)
    pt = jnp.pad(jnp.concatenate([p, p], axis=1), ((0, 2), (0, 0)))
    half = (lax.broadcasted_iota(jnp.int32, (8, 128), 1) >> 6) == par
    pt = jnp.where(half, pt, 0.0)
    par1 = par.reshape(1)
    own, oth = gather_all(jnp.concatenate([tiles(f), pt], axis=0))
    pfull = pt + lax.ppermute(pt, "c", [(0, 1), (1, 0)])

    def reduce_gen(gen):
        got = lax.all_to_all(gen, CHIPS, 0, 0, tiled=True)
        got = jnp.sum(got, axis=0)
        return (got + lax.ppermute(got, "c", [(0, 1), (1, 0)])) / 16.0

    def add_br(c):
        return c + lax.ppermute(c, "br", [(0, 1), (1, 0)])

    c1, gen1 = phase(True, par1, own, oth, f, win, idx, q, g)
    gen1 = reduce_gen(gen1)
    f2 = f + 0.1 * add_br(c1)
    p2 = pfull + 0.1 * gen1
    own, oth = gather_all(jnp.concatenate([tiles(f2), p2], axis=0))
    c2, gen2 = phase(False, par1, own, oth, f2, win, idx, q, g)
    gen2 = reduce_gen(gen2)
    gen2 = jnp.where(par == 0, gen2[:6, :64], gen2[:6, 64:])
    return add_br(c2), gen2


def solution(mesh):
    fine = Mesh(mesh.devices.reshape(4, 2, 4, 2, 2), ("y", "zl", "x", "c", "br"))
    ka = ("y", "zl", "x", "c")
    in_specs = (
        P(None, ka), P("br", ka), P(None, "br", None, None, ka), P(None, ka), P(None, ka), P(None, ka),
    )
    out_specs = (P(None, ka), P("br", ka))
    return jax.shard_map(on_device, mesh=fine, in_specs=in_specs, out_specs=out_specs, check_vma=False)
```

```python
import functools
import jax
import jax.numpy as jnp
from jax import lax
from jax.experimental import pallas as pl
from jax.experimental.pallas import tpu as pltpu
from jax.sharding import Mesh, PartitionSpec as P

F32 = jnp.float32
BF16 = jnp.bfloat16
I32 = jnp.int32
CHIPS = ("y", "zl", "x")
SWAP = [(0, 1), (1, 0)]


def split2(a):
    hi = a.astype(BF16)
    return hi, (a - hi.astype(F32)).astype(BF16)


def rows_are(sel, index):
    io = lax.broadcasted_iota(I32, (sel, index.shape[1]), 0)
    return jnp.where(io == index, 1.0, 0.0).astype(BF16)


def table_parts(tab_ref, t2):
    for kb in range(4):
        for part, val in enumerate(split2(tab_ref[:, kb * 8 : (kb + 1) * 8, :])):
            t2[:, part, :, kb * 128 : (kb + 1) * 128] = val


def pick(count, index, x):
    index = jnp.broadcast_to(index, (8, 512))
    hi = jnp.zeros((8, 512), F32)
    lo = jnp.zeros((8, 512), F32)
    for r in range(count):
        hit = index == r
        hi = jnp.where(hit, x[r * 16 : r * 16 + 8, :], hi)
        lo = jnp.where(hit, x[r * 16 + 8 : r * 16 + 16, :], lo)
    return hi + lo


def look_up(t2, x, row, parity):
    lo = jnp.where(((row >> 9) & 1) == parity, row & 511, -1)
    x[...] = jnp.dot(t2.reshape(512, 512)[...], rows_are(512, lo), preferred_element_type=F32)
    return pick(32, row >> 10, x)


def start_kernel(par_ref, f_ref, p_ref, idx_ref, q_ref, win_ref, send_ref, f_out, idx_out, q_out, win_out):
    p = p_ref[...]
    lane = lax.broadcasted_iota(I32, (6, 128), 1)
    p = jnp.where((lane >> 6) == par_ref[0], jnp.concatenate([p, p], axis=1), 0.0)
    for kb in range(4):
        tile = f_ref[:, kb * 128 : (kb + 1) * 128]
        send_ref[:, kb * 8 : (kb + 1) * 8, :] = jnp.broadcast_to(tile[None], (32, 8, 128))
    p = jnp.concatenate([p, jnp.zeros((2, 128), F32)], axis=0)
    send_ref[:, 32:40, :] = jnp.broadcast_to(p[None], (32, 8, 128))
    f_out[...] = f_ref[...]
    idx_out[...] = idx_ref[...]
    q_out[...] = q_ref[...]
    win_out[...] = win_ref[...]


def own_kernel(par_ref, own_ref, idx_ref, e_ref, t2, xa, xb):
    par = par_ref[0]
    table_parts(own_ref, t2)

    def step(i, _):
        for k, x in enumerate((xa, xb)):
            s = i * 2 + k
            e_ref[s] = look_up(t2, x, idx_ref[pl.ds(s, 1), :], par)
        return 0

    lax.fori_loop(0, 8, step, 0)


def main_kernel(
    merge, par_ref, own_ref, oth_ref, e_ref, f_ref, win_ref, idx_ref, q_ref, g_hbm,
    c_ref, gen_ref, g_ref, t2, p2, xa, ya, xb, yb, ea, wa, va, eb, wb, vb, fw, cacc, gacc, sems,
):
    for s in range(16):
        pltpu.make_async_copy(g_hbm.at[s], g_ref.at[s], sems.at[s]).start()
    other = 1 - par_ref[0]
    table_parts(oth_ref, t2)
    ph = own_ref[:, 32:40, :]
    if merge:
        ph = ph + oth_ref[:, 32:40, :]
    ph = ph.reshape(16, 2, 8, 128)
    for h in range(2):
        for part, val in enumerate(split2(ph[:, h])):
            p2[:, part, :, h * 128 : (h + 1) * 128] = val
    for m in range(8):
        fm = jnp.broadcast_to(f_ref[m : m + 1, :], (8, 512))
        wm = jnp.broadcast_to(win_ref[m : m + 1, :].astype(F32), (8, 512))
        fw[0, m] = wm * (1.0 - fm)
        fw[1, m] = wm
        fw[2, m] = fm
    cacc[...] = jnp.zeros_like(cacc)
    gacc[...] = jnp.zeros_like(gacc)
    va[...] = jnp.zeros_like(va)
    vb[...] = jnp.zeros_like(vb)

    def look(s, x, y, e_s, w_s):
        qrow = q_ref[pl.ds(s, 1), :]
        y[...] = jnp.dot(
            p2.reshape(256, 256)[...], rows_are(256, qrow & 255), preferred_element_type=F32
        )
        e_s[...] = look_up(t2, x, idx_ref[pl.ds(s, 1), :], other) + e_ref[s]
        w_s[...] = pick(16, qrow >> 8, y)

    def contract(s, e_s, w_s, v_s):
        pltpu.make_async_copy(g_hbm.at[s], g_ref.at[s], sems.at[s]).wait()
        for kb in range(4):
            cols = slice(kb * 128, (kb + 1) * 128)
            e = e_s[:, cols]
            d1, d2, ca = [], [], []
            for m in range(8):
                d1.append(fw[0, m, :, cols] * e)
                d2.append(fw[1, m, :, cols] * (e - fw[2, m, :, cols]))
                ca.append(cacc[m, :, cols])
            for u in range(6):
                wu = jnp.broadcast_to(w_s[u : u + 1, cols], (8, 128))
                ga = None
                for m in range(8):
                    tm = g_ref[s, u, m, :, cols].astype(F32) * (d1[m] + wu * d2[m])
                    ca[m] = ca[m] + tm
                    ga = tm if ga is None else ga + tm
                v_s[u : u + 1, cols] = jnp.sum(ga, axis=0, keepdims=True)
            for m in range(8):
                cacc[m, :, cols] = ca[m]

    def scatter(s, v_s):
        qrow = q_ref[pl.ds(s, 1), :]
        v = v_s[...]
        v1 = v.astype(BF16).astype(F32)
        v2 = v - v1
        hm = lax.broadcasted_iota(I32, (16, 8, 512), 0) == (qrow >> 8)[None]
        a = [
            jnp.where(hm, jnp.broadcast_to(vv[None], (16, 8, 512)), 0.0).astype(BF16).reshape(128, 512)
            for vv in (v1, v2)
        ]
        gacc[...] += lax.dot_general(
            jnp.concatenate(a, axis=0), rows_are(256, qrow & 255), (((1,), (1,)), ((), ())),
            preferred_element_type=F32,
        )

    look(0, xa, ya, ea, wa)

    def step(i, _):
        s = 2 * i
        look(s + 1, xb, yb, eb, wb)
        scatter(jnp.maximum(s - 1, 0), vb)
        contract(s, ea, wa, va)
        look(jnp.minimum(s + 2, 15), xa, ya, ea, wa)
        scatter(s, va)
        contract(s + 1, eb, wb, vb)
        return 0

    lax.fori_loop(0, 8, step, 0)
    scatter(15, vb)
    for m in range(8):
        c_ref[m : m + 1, :] = jnp.sum(cacc[m], axis=0, keepdims=True)
    gs = (gacc[0:128] + gacc[128:256]).reshape(16, 8, 256)
    for h in range(2):
        gen_ref[:, h] = gs[:, :, h * 128 : (h + 1) * 128]


VM = pl.BlockSpec(memory_space=pltpu.VMEM)
SM = pl.BlockSpec(memory_space=pltpu.SMEM)


def in_vmem(a):
    return pltpu.with_memory_space_constraint(a, pltpu.VMEM)


def in_hbm(a):
    return pltpu.with_memory_space_constraint(a, pltpu.HBM)


def phase(merge, par, own, oth, f, win, idx, q, g):
    scratch = [
        pltpu.VMEM((32, 2, 8, 512), BF16),
        pltpu.VMEM((512, 512), F32),
        pltpu.VMEM((512, 512), F32),
    ]
    own, oth, f, win, idx, q = map(in_vmem, (own, oth, f, win, idx, q))
    g = in_hbm(g)
    e = pl.pallas_call(
        own_kernel,
        out_shape=pltpu.VMEM((16, 8, 512), F32),
        in_specs=[SM, VM, VM],
        out_specs=VM,
        scratch_shapes=scratch,
        compiler_params=pltpu.CompilerParams(vmem_limit_bytes=12 << 20),
        name="own",
    )(par, own, idx)
    c, gen = pl.pallas_call(
        functools.partial(main_kernel, merge),
        out_shape=(pltpu.VMEM((8, 512), F32), pltpu.VMEM((16, 2, 8, 128), F32)),
        in_specs=[SM] + [VM] * 7 + [pl.BlockSpec(memory_space=pltpu.HBM)],
        out_specs=(VM, VM),
        scratch_shapes=[
            pltpu.VMEM((16, 6, 8, 8, 512), BF16),
            pltpu.VMEM((32, 2, 8, 512), BF16),
            pltpu.VMEM((16, 2, 8, 256), BF16),
            *([pltpu.VMEM((512, 512), F32), pltpu.VMEM((256, 512), F32)] * 2),
            *([pltpu.VMEM((8, 512), F32)] * 6),
            pltpu.VMEM((3, 8, 8, 512), F32),
            pltpu.VMEM((8, 8, 512), F32),
            pltpu.VMEM((256, 256), F32),
            pltpu.SemaphoreType.DMA((16,)),
        ],
        compiler_params=pltpu.CompilerParams(vmem_limit_bytes=24 << 20),
        name="main",
    )(par, own, oth, in_vmem(e), f, win, idx, q, g)
    return c, gen.reshape(32, 8, 128)


def tiles(f):
    return f.reshape(8, 4, 128).transpose(1, 0, 2).reshape(32, 128)


def gather_all(send):
    own = lax.all_to_all(send, CHIPS, 0, 0, tiled=True)
    return own, lax.ppermute(own, "c", SWAP)


def on_device(f, p, g, idx, q, win):
    par = lax.axis_index("c").astype(I32)
    par1 = par.reshape(1)
    f, p, idx, q, win = map(in_hbm, (f, p, idx, q, win))
    send, f, idx, q, win = pl.pallas_call(
        start_kernel,
        out_shape=(
            pltpu.VMEM((32, 40, 128), F32), pltpu.VMEM((8, 512), F32), pltpu.VMEM((16, 512), I32),
            pltpu.VMEM((16, 512), I32), pltpu.VMEM((8, 512), I32),
        ),
        in_specs=[SM] + [VM] * 5,
        out_specs=(VM,) * 5,
        compiler_params=pltpu.CompilerParams(vmem_limit_bytes=8 << 20),
        name="start",
    )(par1, f, p, idx, q, win)
    own, oth = gather_all(send)
    pt = send[0, 32:40]
    pfull = pt + lax.ppermute(pt, "c", SWAP)

    def reduce_gen(gen):
        got = lax.all_to_all(gen, CHIPS, 0, 0, tiled=True)
        got = jnp.sum(got, axis=0)
        return (got + lax.ppermute(got, "c", SWAP)) / 16.0

    def add_br(c):
        return c + lax.ppermute(c, "br", SWAP)

    c1, gen1 = phase(True, par1, own, oth, f, win, idx, q, g)
    gen1 = reduce_gen(gen1)
    f2 = f + 0.1 * add_br(c1)
    p2 = pfull + 0.1 * gen1
    chunk = jnp.concatenate([tiles(f2), p2], axis=0)
    own, oth = gather_all(jnp.broadcast_to(chunk[None], (32, 40, 128)))
    c2, gen2 = phase(False, par1, own, oth, f2, win, idx, q, g)
    gen2 = reduce_gen(gen2)
    gen2 = jnp.where(par == 0, gen2[:6, :64], gen2[:6, 64:])
    return add_br(c2), gen2


def solution(mesh):
    fine = Mesh(mesh.devices.reshape(4, 2, 4, 2, 2), ("y", "zl", "x", "c", "br"))
    ka = ("y", "zl", "x", "c")
    in_specs = (
        P(None, ka), P("br", ka), P(None, "br", None, None, ka), P(None, ka), P(None, ka), P(None, ka),
    )
    out_specs = (P(None, ka), P("br", ka))
    return jax.shard_map(on_device, mesh=fine, in_specs=in_specs, out_specs=out_specs, check_vma=False)
```

```python
import functools
import jax
import jax.numpy as jnp
from jax import lax
from jax.experimental import pallas as pl
from jax.experimental.pallas import tpu as pltpu
from jax.sharding import Mesh, PartitionSpec as P


F32 = jnp.float32
BF16 = jnp.bfloat16
I32 = jnp.int32
CHIPS = ("y", "zl", "x")
SWAP = [(0, 1), (1, 0)]


def split2(a):
    hi = a.astype(BF16)
    return hi, (a - hi.astype(F32)).astype(BF16)


def rows_are(sel, index):
    io = lax.broadcasted_iota(I32, (sel, index.shape[1]), 0)
    return jnp.where(io == index, 1.0, 0.0).astype(BF16)


def table_parts(tab_ref, t2):
    for kb in range(4):
        for part, val in enumerate(split2(tab_ref[:, kb * 8 : (kb + 1) * 8, :])):
            t2[:, part, :, kb * 128 : (kb + 1) * 128] = val


def pick(count, index, x):
    index = jnp.broadcast_to(index, (8, 512))
    hi = jnp.zeros((8, 512), F32)
    lo = jnp.zeros((8, 512), F32)
    for r in range(count):
        hit = index == r
        hi = jnp.where(hit, x[r * 16 : r * 16 + 8, :], hi)
        lo = jnp.where(hit, x[r * 16 + 8 : r * 16 + 16, :], lo)
    return hi + lo


def look_up(t2, x, row, parity):
    lo = jnp.where(((row >> 9) & 1) == parity, row & 511, -1)
    x[...] = jnp.dot(t2.reshape(512, 512)[...], rows_are(512, lo), preferred_element_type=F32)
    return pick(32, row >> 10, x)


def start_kernel(par_ref, f_ref, p_ref, idx_ref, q_ref, win_ref, send_ref, f_out, idx_out, q_out, win_out):
    p = p_ref[...]
    lane = lax.broadcasted_iota(I32, (6, 128), 1)
    p = jnp.where((lane >> 6) == (par_ref[0] & 1), jnp.concatenate([p, p], axis=1), 0.0)
    for kb in range(4):
        tile = f_ref[:, kb * 128 : (kb + 1) * 128]
        send_ref[:, kb * 8 : (kb + 1) * 8, :] = jnp.broadcast_to(tile[None], (32, 8, 128))
    p = jnp.concatenate([p, jnp.zeros((2, 128), F32)], axis=0)
    send_ref[:, 32:40, :] = jnp.broadcast_to(p[None], (32, 8, 128))
    f_out[...] = f_ref[...]
    idx_out[...] = idx_ref[...]
    q_out[...] = q_ref[...]
    win_out[...] = win_ref[...]


def own_kernel(par_ref, own_ref, idx_ref, e_ref, t2, xa, xb):
    par = par_ref[0] & 1
    table_parts(own_ref, t2)

    def step(i, _):
        for k, x in enumerate((xa, xb)):
            s = i * 2 + k
            e_ref[s] = look_up(t2, x, idx_ref[pl.ds(s, 1), :], par)
        return 0

    lax.fori_loop(0, 8, step, 0)


def main_kernel(
    merge, par_ref, own_ref, oth_ref, e_ref, f_ref, win_ref, idx_ref, q_ref, g_hbm,
    c_ref, gen_ref, pc_ref, g_ref, t2, p2, xa, ya, xb, yb, ea, wa, va, eb, wb, vb, fw, cacc, gacc, sems,
):
    for s in range(16):
        pltpu.make_async_copy(g_hbm.at[s], g_ref.at[s], sems.at[s]).start()
    other = 1 - (par_ref[0] & 1)
    table_parts(oth_ref, t2)
    ph = own_ref[:, 32:40, :]
    if merge:
        ph = ph + oth_ref[:, 32:40, :]
    pc = own_ref[par_ref[0] >> 1, 32:40, :]
    if merge:
        pc = pc + oth_ref[par_ref[0] >> 1, 32:40, :]
    pc_ref[...] = pc
    ph = ph.reshape(16, 2, 8, 128)
    for h in range(2):
        for part, val in enumerate(split2(ph[:, h])):
            p2[:, part, :, h * 128 : (h + 1) * 128] = val
    for m in range(8):
        fm = jnp.broadcast_to(f_ref[m : m + 1, :], (8, 512))
        wm = jnp.broadcast_to(win_ref[m : m + 1, :].astype(F32), (8, 512))
        fw[0, m] = wm * (1.0 - fm)
        fw[1, m] = wm
        fw[2, m] = fm
    cacc[...] = jnp.zeros_like(cacc)
    gacc[...] = jnp.zeros_like(gacc)
    va[...] = jnp.zeros_like(va)
    vb[...] = jnp.zeros_like(vb)

    def look(s, x, y, e_s, w_s):
        qrow = q_ref[pl.ds(s, 1), :]
        y[...] = jnp.dot(
            p2.reshape(256, 256)[...], rows_are(256, qrow & 255), preferred_element_type=F32
        )
        e_s[...] = look_up(t2, x, idx_ref[pl.ds(s, 1), :], other) + e_ref[s]
        w_s[...] = pick(16, qrow >> 8, y)

    def contract(s, e_s, w_s, v_s):
        pltpu.make_async_copy(g_hbm.at[s], g_ref.at[s], sems.at[s]).wait()
        for kb in range(4):
            cols = slice(kb * 128, (kb + 1) * 128)
            e = e_s[:, cols]
            d1, d2, ca = [], [], []
            for m in range(8):
                d1.append(fw[0, m, :, cols] * e)
                d2.append(fw[1, m, :, cols] * (e - fw[2, m, :, cols]))
                ca.append(cacc[m, :, cols])
            for u in range(6):
                wu = jnp.broadcast_to(w_s[u : u + 1, cols], (8, 128))
                ga = None
                for m in range(8):
                    tm = g_ref[s, u, m, :, cols].astype(F32) * (d1[m] + wu * d2[m])
                    ca[m] = ca[m] + tm
                    ga = tm if ga is None else ga + tm
                v_s[u : u + 1, cols] = jnp.sum(ga, axis=0, keepdims=True)
            for m in range(8):
                cacc[m, :, cols] = ca[m]

    def scatter(s, v_s):
        qrow = q_ref[pl.ds(s, 1), :]
        v = v_s[...]
        v1 = v.astype(BF16).astype(F32)
        v2 = v - v1
        hm = lax.broadcasted_iota(I32, (16, 8, 512), 0) == (qrow >> 8)[None]
        a = [
            jnp.where(hm, jnp.broadcast_to(vv[None], (16, 8, 512)), 0.0).astype(BF16).reshape(128, 512)
            for vv in (v1, v2)
        ]
        gacc[...] += lax.dot_general(
            jnp.concatenate(a, axis=0), rows_are(256, qrow & 255), (((1,), (1,)), ((), ())),
            preferred_element_type=F32,
        )

    look(0, xa, ya, ea, wa)

    def step(i, _):
        s = 2 * i
        look(s + 1, xb, yb, eb, wb)
        scatter(jnp.maximum(s - 1, 0), vb)
        contract(s, ea, wa, va)
        look(jnp.minimum(s + 2, 15), xa, ya, ea, wa)
        scatter(s, va)
        contract(s + 1, eb, wb, vb)
        return 0

    lax.fori_loop(0, 8, step, 0)
    scatter(15, vb)
    for m in range(8):
        c_ref[m : m + 1, :] = jnp.sum(cacc[m], axis=0, keepdims=True)
    gs = (gacc[0:128] + gacc[128:256]).reshape(16, 8, 256)
    for h in range(2):
        gen_ref[:, h] = gs[:, :, h * 128 : (h + 1) * 128]


VM = pl.BlockSpec(memory_space=pltpu.VMEM)
SM = pl.BlockSpec(memory_space=pltpu.SMEM)


def in_vmem(a):
    return pltpu.with_memory_space_constraint(a, pltpu.VMEM)


def in_hbm(a):
    return pltpu.with_memory_space_constraint(a, pltpu.HBM)


def phase(merge, par, own, oth, f, win, idx, q, g):
    scratch = [
        pltpu.VMEM((32, 2, 8, 512), BF16),
        pltpu.VMEM((512, 512), F32),
        pltpu.VMEM((512, 512), F32),
    ]
    own, oth, f, win, idx, q = map(in_vmem, (own, oth, f, win, idx, q))
    g = in_hbm(g)
    e = pl.pallas_call(
        own_kernel,
        out_shape=pltpu.VMEM((16, 8, 512), F32),
        in_specs=[SM, VM, VM],
        out_specs=VM,
        scratch_shapes=scratch,
        compiler_params=pltpu.CompilerParams(vmem_limit_bytes=12 << 20),
        name="own",
    )(par, own, idx)
    c, gen, pc = pl.pallas_call(
        functools.partial(main_kernel, merge),
        out_shape=(pltpu.VMEM((8, 512), F32), pltpu.VMEM((16, 2, 8, 128), F32), pltpu.VMEM((8, 128), F32)),
        in_specs=[SM] + [VM] * 7 + [pl.BlockSpec(memory_space=pltpu.HBM)],
        out_specs=(VM, VM, VM),
        scratch_shapes=[
            pltpu.VMEM((16, 6, 8, 8, 512), BF16),
            pltpu.VMEM((32, 2, 8, 512), BF16),
            pltpu.VMEM((16, 2, 8, 256), BF16),
            *([pltpu.VMEM((512, 512), F32), pltpu.VMEM((256, 512), F32)] * 2),
            *([pltpu.VMEM((8, 512), F32)] * 6),
            pltpu.VMEM((3, 8, 8, 512), F32),
            pltpu.VMEM((8, 8, 512), F32),
            pltpu.VMEM((256, 256), F32),
            pltpu.SemaphoreType.DMA((16,)),
        ],
        compiler_params=pltpu.CompilerParams(vmem_limit_bytes=24 << 20),
        name="main",
    )(par, own, oth, in_vmem(e), f, win, idx, q, g)
    return c, gen.reshape(32, 8, 128), pc


def tiles(f):
    return f.reshape(8, 4, 128).transpose(1, 0, 2).reshape(32, 128)


def gather_all(send):
    own = lax.all_to_all(send, CHIPS, 0, 0, tiled=True)
    return own, lax.ppermute(own, "c", SWAP)


def on_device(f, p, g, idx, q, win):
    par = lax.axis_index("c").astype(I32)
    chip = (lax.axis_index("y") * 2 + lax.axis_index("zl")) * 4 + lax.axis_index("x")
    par1 = (chip.astype(I32) * 2 + par).reshape(1)
    f, p, idx, q, win = map(in_hbm, (f, p, idx, q, win))
    send, f, idx, q, win = pl.pallas_call(
        start_kernel,
        out_shape=(
            pltpu.VMEM((32, 40, 128), F32), pltpu.VMEM((8, 512), F32), pltpu.VMEM((16, 512), I32),
            pltpu.VMEM((16, 512), I32), pltpu.VMEM((8, 512), I32),
        ),
        in_specs=[SM] + [VM] * 5,
        out_specs=(VM,) * 5,
        compiler_params=pltpu.CompilerParams(vmem_limit_bytes=8 << 20),
        name="start",
    )(par1, f, p, idx, q, win)
    own, oth = gather_all(send)

    def reduce_gen(gen):
        got = lax.all_to_all(gen, CHIPS, 0, 0, tiled=True)
        got = jnp.sum(got, axis=0)
        return (got + lax.ppermute(got, "c", SWAP)) / 16.0

    def add_br(c):
        other = lax.ppermute(c, "br", SWAP)
        return c + other

    c1, gen1, pc = phase(True, par1, own, oth, f, win, idx, q, g)
    gen1 = reduce_gen(gen1)
    f2 = f + 0.1 * add_br(c1)
    p2 = pc + 0.1 * gen1
    chunk = jnp.concatenate([tiles(f2), p2], axis=0)
    own, oth = gather_all(jnp.broadcast_to(chunk[None], (32, 40, 128)))
    c2, gen2, _ = phase(False, par1, own, oth, f2, win, idx, q, g)
    gen2 = reduce_gen(gen2)
    gen2 = jnp.where(par == 0, gen2[:6, :64], gen2[:6, 64:])
    return add_br(c2), gen2


def solution(mesh):
    fine = Mesh(mesh.devices.reshape(4, 2, 4, 2, 2), ("y", "zl", "x", "c", "br"))
    ka = ("y", "zl", "x", "c")
    in_specs = (
        P(None, ka), P("br", ka), P(None, "br", None, None, ka), P(None, ka), P(None, ka), P(None, ka),
    )
    out_specs = (P(None, ka), P("br", ka))
    return jax.shard_map(on_device, mesh=fine, in_specs=in_specs, out_specs=out_specs, check_vma=False)
```

```python
import functools
import jax
import jax.numpy as jnp
from jax import lax
from jax.experimental import pallas as pl
from jax.experimental.pallas import tpu as pltpu
from jax.sharding import Mesh, PartitionSpec as P


F32 = jnp.float32
BF16 = jnp.bfloat16
I32 = jnp.int32
CHIPS = ("y", "zl", "x")
SWAP = [(0, 1), (1, 0)]


def split2(a):
    hi = a.astype(BF16)
    return hi, (a - hi.astype(F32)).astype(BF16)


def rows_are(sel, index):
    io = lax.broadcasted_iota(I32, (sel, index.shape[1]), 0)
    return jnp.where(io == index, 1.0, 0.0).astype(BF16)


def table_parts(tab_ref, t2):
    for kb in range(4):
        for part, val in enumerate(split2(tab_ref[:, kb * 8 : (kb + 1) * 8, :])):
            t2[:, part, :, kb * 128 : (kb + 1) * 128] = val


def pick(count, index, x):
    index = jnp.broadcast_to(index, (8, 512))
    hi = jnp.zeros((8, 512), F32)
    lo = jnp.zeros((8, 512), F32)
    for r in range(count):
        hit = index == r
        hi = jnp.where(hit, x[r * 16 : r * 16 + 8, :], hi)
        lo = jnp.where(hit, x[r * 16 + 8 : r * 16 + 16, :], lo)
    return hi + lo


def look_up(t2, x, row, parity):
    lo = jnp.where(((row >> 9) & 1) == parity, row & 511, -1)
    x[...] = jnp.dot(t2.reshape(512, 512)[...], rows_are(512, lo), preferred_element_type=F32)
    return pick(32, row >> 10, x)


def start_kernel(par_ref, f_ref, p_ref, idx_ref, q_ref, win_ref, send_ref, f_out, idx_out, q_out, win_out):
    p = p_ref[...]
    lane = lax.broadcasted_iota(I32, (6, 128), 1)
    p = jnp.where((lane >> 6) == (par_ref[0] & 1), jnp.concatenate([p, p], axis=1), 0.0)
    for kb in range(4):
        tile = f_ref[:, kb * 128 : (kb + 1) * 128]
        send_ref[:, kb * 8 : (kb + 1) * 8, :] = jnp.broadcast_to(tile[None], (32, 8, 128))
    p = jnp.concatenate([p, jnp.zeros((2, 128), F32)], axis=0)
    send_ref[:, 32:40, :] = jnp.broadcast_to(p[None], (32, 8, 128))
    f_out[...] = f_ref[...]
    idx_out[...] = idx_ref[...]
    q_out[...] = q_ref[...]
    win_out[...] = win_ref[...]


def own_kernel(par_ref, own_ref, idx_ref, e_ref, t2, xa, xb):
    par = par_ref[0] & 1
    table_parts(own_ref, t2)

    def step(i, _):
        for k, x in enumerate((xa, xb) * 8):
            s = i * 16 + k
            e_ref[s] = look_up(t2, x, idx_ref[pl.ds(s, 1), :], par)
        return 0

    lax.fori_loop(0, 1, step, 0)


def main_kernel(
    merge, par_ref, own_ref, oth_ref, e_ref, f_ref, win_ref, idx_ref, q_ref, g_hbm,
    c_ref, gen_ref, pc_ref, g_ref, t2, p2, xa, ya, xb, yb, ea, wa, va, eb, wb, vb, fw, cacc, gacc, sems,
):
    for s in range(16):
        pltpu.make_async_copy(g_hbm.at[s], g_ref.at[s], sems.at[s]).start()
    other = 1 - (par_ref[0] & 1)
    table_parts(oth_ref, t2)
    ph = own_ref[:, 32:40, :]
    if merge:
        ph = ph + oth_ref[:, 32:40, :]
    pc = own_ref[par_ref[0] >> 1, 32:40, :]
    if merge:
        pc = pc + oth_ref[par_ref[0] >> 1, 32:40, :]
    pc_ref[...] = pc
    ph = ph.reshape(16, 2, 8, 128)
    for h in range(2):
        for part, val in enumerate(split2(ph[:, h])):
            p2[:, part, :, h * 128 : (h + 1) * 128] = val
    for m in range(8):
        fm = jnp.broadcast_to(f_ref[m : m + 1, :], (8, 512))
        wm = jnp.broadcast_to(win_ref[m : m + 1, :].astype(F32), (8, 512))
        fw[0, m] = wm * (1.0 - fm)
        fw[1, m] = wm
        fw[2, m] = fm
    cacc[...] = jnp.zeros_like(cacc)
    gacc[...] = jnp.zeros_like(gacc)
    va[...] = jnp.zeros_like(va)
    vb[...] = jnp.zeros_like(vb)

    def look(s, x, y, e_s, w_s):
        qrow = q_ref[pl.ds(s, 1), :]
        y[...] = jnp.dot(
            p2.reshape(256, 256)[...], rows_are(256, qrow & 255), preferred_element_type=F32
        )
        e_s[...] = look_up(t2, x, idx_ref[pl.ds(s, 1), :], other) + e_ref[s]
        w_s[...] = pick(16, qrow >> 8, y)

    def contract(s, e_s, w_s, v_s):
        pltpu.make_async_copy(g_hbm.at[s], g_ref.at[s], sems.at[s]).wait()
        for kb in range(4):
            cols = slice(kb * 128, (kb + 1) * 128)
            e = e_s[:, cols]
            d1, d2, ca = [], [], []
            for m in range(8):
                d1.append(fw[0, m, :, cols] * e)
                d2.append(fw[1, m, :, cols] * (e - fw[2, m, :, cols]))
                ca.append(cacc[m, :, cols])
            for u in range(6):
                wu = jnp.broadcast_to(w_s[u : u + 1, cols], (8, 128))
                ga = None
                for m in range(8):
                    tm = g_ref[s, u, m, :, cols].astype(F32) * (d1[m] + wu * d2[m])
                    ca[m] = ca[m] + tm
                    ga = tm if ga is None else ga + tm
                v_s[u : u + 1, cols] = jnp.sum(ga, axis=0, keepdims=True)
            for m in range(8):
                cacc[m, :, cols] = ca[m]

    def scatter(s, v_s):
        qrow = q_ref[pl.ds(s, 1), :]
        v = v_s[...]
        v1 = v.astype(BF16).astype(F32)
        v2 = v - v1
        hm = lax.broadcasted_iota(I32, (16, 8, 512), 0) == (qrow >> 8)[None]
        a = [
            jnp.where(hm, jnp.broadcast_to(vv[None], (16, 8, 512)), 0.0).astype(BF16).reshape(128, 512)
            for vv in (v1, v2)
        ]
        gacc[...] += lax.dot_general(
            jnp.concatenate(a, axis=0), rows_are(256, qrow & 255), (((1,), (1,)), ((), ())),
            preferred_element_type=F32,
        )

    look(0, xa, ya, ea, wa)

    def step(i, _):
        s = 8 * i
        look(s + 1, xb, yb, eb, wb)
        scatter(jnp.maximum(s - 1, 0), vb)
        contract(s, ea, wa, va)
        look(s + 2, xa, ya, ea, wa)
        scatter(s, va)
        contract(s + 1, eb, wb, vb)
        look(s + 3, xb, yb, eb, wb)
        scatter(s + 1, vb)
        contract(s + 2, ea, wa, va)
        look(s + 4, xa, ya, ea, wa)
        scatter(s + 2, va)
        contract(s + 3, eb, wb, vb)
        look(s + 5, xb, yb, eb, wb)
        scatter(s + 3, vb)
        contract(s + 4, ea, wa, va)
        look(s + 6, xa, ya, ea, wa)
        scatter(s + 4, va)
        contract(s + 5, eb, wb, vb)
        look(s + 7, xb, yb, eb, wb)
        scatter(s + 5, vb)
        contract(s + 6, ea, wa, va)
        look(jnp.minimum(s + 8, 15), xa, ya, ea, wa)
        scatter(s + 6, va)
        contract(s + 7, eb, wb, vb)
        return 0

    lax.fori_loop(0, 2, step, 0)
    scatter(15, vb)
    for m in range(8):
        c_ref[m : m + 1, :] = jnp.sum(cacc[m], axis=0, keepdims=True)
    gs = (gacc[0:128] + gacc[128:256]).reshape(16, 8, 256)
    for h in range(2):
        gen_ref[:, h] = gs[:, :, h * 128 : (h + 1) * 128]


VM = pl.BlockSpec(memory_space=pltpu.VMEM)
SM = pl.BlockSpec(memory_space=pltpu.SMEM)


def in_vmem(a):
    return pltpu.with_memory_space_constraint(a, pltpu.VMEM)


def in_hbm(a):
    return pltpu.with_memory_space_constraint(a, pltpu.HBM)


def phase(merge, par, own, oth, f, win, idx, q, g):
    scratch = [
        pltpu.VMEM((32, 2, 8, 512), BF16),
        pltpu.VMEM((512, 512), F32),
        pltpu.VMEM((512, 512), F32),
    ]
    own, oth, f, win, idx, q = map(in_vmem, (own, oth, f, win, idx, q))
    g = in_hbm(g)
    e = pl.pallas_call(
        own_kernel,
        out_shape=pltpu.VMEM((16, 8, 512), F32),
        in_specs=[SM, VM, VM],
        out_specs=VM,
        scratch_shapes=scratch,
        compiler_params=pltpu.CompilerParams(vmem_limit_bytes=12 << 20),
        name="own",
    )(par, own, idx)
    c, gen, pc = pl.pallas_call(
        functools.partial(main_kernel, merge),
        out_shape=(pltpu.VMEM((8, 512), F32), pltpu.VMEM((16, 2, 8, 128), F32), pltpu.VMEM((8, 128), F32)),
        in_specs=[SM] + [VM] * 7 + [pl.BlockSpec(memory_space=pltpu.HBM)],
        out_specs=(VM, VM, VM),
        scratch_shapes=[
            pltpu.VMEM((16, 6, 8, 8, 512), BF16),
            pltpu.VMEM((32, 2, 8, 512), BF16),
            pltpu.VMEM((16, 2, 8, 256), BF16),
            *([pltpu.VMEM((512, 512), F32), pltpu.VMEM((256, 512), F32)] * 2),
            *([pltpu.VMEM((8, 512), F32)] * 6),
            pltpu.VMEM((3, 8, 8, 512), F32),
            pltpu.VMEM((8, 8, 512), F32),
            pltpu.VMEM((256, 256), F32),
            pltpu.SemaphoreType.DMA((16,)),
        ],
        compiler_params=pltpu.CompilerParams(vmem_limit_bytes=24 << 20),
        name="main",
    )(par, own, oth, in_vmem(e), f, win, idx, q, g)
    return c, gen.reshape(32, 8, 128), pc


def tiles(f):
    return f.reshape(8, 4, 128).transpose(1, 0, 2).reshape(32, 128)


def gather_all(send):
    own = lax.all_to_all(send, CHIPS, 0, 0, tiled=True)
    return own, lax.ppermute(own, "c", SWAP)


def on_device(f, p, g, idx, q, win):
    par = lax.axis_index("c").astype(I32)
    chip = (lax.axis_index("y") * 2 + lax.axis_index("zl")) * 4 + lax.axis_index("x")
    par1 = (chip.astype(I32) * 2 + par).reshape(1)
    f, p, idx, q, win = map(in_hbm, (f, p, idx, q, win))
    send, f, idx, q, win = pl.pallas_call(
        start_kernel,
        out_shape=(
            pltpu.VMEM((32, 40, 128), F32), pltpu.VMEM((8, 512), F32), pltpu.VMEM((16, 512), I32),
            pltpu.VMEM((16, 512), I32), pltpu.VMEM((8, 512), I32),
        ),
        in_specs=[SM] + [VM] * 5,
        out_specs=(VM,) * 5,
        compiler_params=pltpu.CompilerParams(vmem_limit_bytes=8 << 20),
        name="start",
    )(par1, f, p, idx, q, win)
    own, oth = gather_all(send)

    def reduce_gen(gen):
        got = lax.all_to_all(gen, CHIPS, 0, 0, tiled=True)
        got = jnp.sum(got, axis=0)
        return (got + lax.ppermute(got, "c", SWAP)) / 16.0

    def add_br(c):
        other = lax.ppermute(c, "br", SWAP)
        return c + other

    c1, gen1, pc = phase(True, par1, own, oth, f, win, idx, q, g)
    gen1 = reduce_gen(gen1)
    f2 = f + 0.1 * add_br(c1)
    p2 = pc + 0.1 * gen1
    chunk = jnp.concatenate([tiles(f2), p2], axis=0)
    own, oth = gather_all(jnp.broadcast_to(chunk[None], (32, 40, 128)))
    c2, gen2, _ = phase(False, par1, own, oth, f2, win, idx, q, g)
    gen2 = reduce_gen(gen2)
    gen2 = jnp.where(par == 0, gen2[:6, :64], gen2[:6, 64:])
    return add_br(c2), gen2


def solution(mesh):
    fine = Mesh(mesh.devices.reshape(4, 2, 4, 2, 2), ("y", "zl", "x", "c", "br"))
    ka = ("y", "zl", "x", "c")
    in_specs = (
        P(None, ka), P("br", ka), P(None, "br", None, None, ka), P(None, ka), P(None, ka), P(None, ka),
    )
    out_specs = (P(None, ka), P("br", ka))
    return jax.shard_map(on_device, mesh=fine, in_specs=in_specs, out_specs=out_specs, check_vma=False)
```

```python
import functools
import jax
import jax.numpy as jnp
from jax import lax
from jax.experimental import pallas as pl
from jax.experimental.pallas import tpu as pltpu
from jax.sharding import Mesh, PartitionSpec as P


F32 = jnp.float32
BF16 = jnp.bfloat16
I32 = jnp.int32
CHIPS = ("y", "zl", "x")
SWAP = [(0, 1), (1, 0)]


def split2(a):
    hi = a.astype(BF16)
    return hi, (a - hi.astype(F32)).astype(BF16)


def rows_are(sel, index):
    io = lax.broadcasted_iota(I32, (sel, index.shape[1]), 0)
    return jnp.where(io == index, 1.0, 0.0).astype(BF16)


def rows_like(io, sel, index):
    blocks = []
    for base in range(0, sel, 256):
        rel = jnp.broadcast_to((index - base).astype(F32), (16, index.shape[1])).astype(BF16)
        for b in range(16):
            row = jnp.concatenate([io[b * 16 : b * 16 + 16, :]] * (index.shape[1] // 128), axis=1)
            blocks.append(jnp.where(row == rel, jnp.ones_like(rel), jnp.zeros_like(rel)))
    return jnp.concatenate(blocks, axis=0)


def table_parts(tab_ref, t2):
    for kb in range(4):
        for part, val in enumerate(split2(tab_ref[:, kb * 8 : (kb + 1) * 8, :])):
            t2[:, part, :, kb * 128 : (kb + 1) * 128] = val


def pick(count, index, x):
    index = jnp.broadcast_to(index, (8, 512))
    hi = jnp.zeros((8, 512), F32)
    lo = jnp.zeros((8, 512), F32)
    for r in range(count):
        hit = index == r
        hi = jnp.where(hit, x[r * 16 : r * 16 + 8, :], hi)
        lo = jnp.where(hit, x[r * 16 + 8 : r * 16 + 16, :], lo)
    return hi + lo


def look_up(t2, x, row, parity, io=None):
    lo = jnp.where(((row >> 9) & 1) == parity, row & 511, -1)
    oh = rows_are(512, lo) if io is None else rows_like(io, 512, lo)
    x[...] = jnp.dot(t2.reshape(512, 512)[...], oh, preferred_element_type=F32)
    return pick(32, row >> 10, x)


def start_kernel(par_ref, f_ref, p_ref, idx_ref, q_ref, win_ref, send_ref, f_out, idx_out, q_out, win_out):
    p = p_ref[...]
    lane = lax.broadcasted_iota(I32, (6, 128), 1)
    p = jnp.where((lane >> 6) == (par_ref[0] & 1), jnp.concatenate([p, p], axis=1), 0.0)
    for kb in range(4):
        tile = f_ref[:, kb * 128 : (kb + 1) * 128]
        send_ref[:, kb * 8 : (kb + 1) * 8, :] = jnp.broadcast_to(tile[None], (32, 8, 128))
    p = jnp.concatenate([p, jnp.zeros((2, 128), F32)], axis=0)
    send_ref[:, 32:40, :] = jnp.broadcast_to(p[None], (32, 8, 128))
    f_out[...] = f_ref[...]
    idx_out[...] = idx_ref[...]
    q_out[...] = q_ref[...]
    win_out[...] = win_ref[...]


def own_kernel(par_ref, own_ref, idx_ref, e_ref, t2, xa, xb):
    par = par_ref[0] & 1
    table_parts(own_ref, t2)

    def step(i, _):
        for k, x in enumerate((xa, xb) * 8):
            s = i * 16 + k
            e_ref[s] = look_up(t2, x, idx_ref[pl.ds(s, 1), :], par)
        return 0

    lax.fori_loop(0, 1, step, 0)


def main_kernel(
    merge, par_ref, own_ref, oth_ref, e_ref, f_ref, win_ref, idx_ref, q_ref, g_hbm,
    c_ref, gen_ref, pc_ref, g_ref, t2, p2, xa, ya, xb, yb, ea, wa, va, eb, wb, vb, fw, cacc, gacc, io, sems,
):
    for s in range(16):
        pltpu.make_async_copy(g_hbm.at[s], g_ref.at[s], sems.at[s]).start()
    other = 1 - (par_ref[0] & 1)
    table_parts(oth_ref, t2)
    ph = own_ref[:, 32:40, :]
    if merge:
        ph = ph + oth_ref[:, 32:40, :]
    pc = own_ref[par_ref[0] >> 1, 32:40, :]
    if merge:
        pc = pc + oth_ref[par_ref[0] >> 1, 32:40, :]
    pc_ref[...] = pc
    ph = ph.reshape(16, 2, 8, 128)
    for h in range(2):
        for part, val in enumerate(split2(ph[:, h])):
            p2[:, part, :, h * 128 : (h + 1) * 128] = val
    for m in range(8):
        fm = jnp.broadcast_to(f_ref[m : m + 1, :], (8, 512))
        wm = jnp.broadcast_to(win_ref[m : m + 1, :].astype(F32), (8, 512))
        fw[0, m] = wm * (1.0 - fm)
        fw[1, m] = wm
        fw[2, m] = fm
    io[...] = lax.broadcasted_iota(I32, (256, 128), 0).astype(F32).astype(BF16)
    cacc[...] = jnp.zeros_like(cacc)
    gacc[...] = jnp.zeros_like(gacc)
    va[...] = jnp.zeros_like(va)
    vb[...] = jnp.zeros_like(vb)

    def look(s, x, y, e_s, w_s):
        qrow = q_ref[pl.ds(s, 1), :]
        y[...] = jnp.dot(
            p2.reshape(256, 256)[...], rows_like(io, 256, qrow & 255), preferred_element_type=F32
        )
        e_s[...] = look_up(t2, x, idx_ref[pl.ds(s, 1), :], other, io) + e_ref[s]
        w_s[...] = pick(16, qrow >> 8, y)

    def contract(s, e_s, w_s, v_s):
        pltpu.make_async_copy(g_hbm.at[s], g_ref.at[s], sems.at[s]).wait()
        for kb in range(4):
            cols = slice(kb * 128, (kb + 1) * 128)
            e = e_s[:, cols]
            d1, d2, ca = [], [], []
            for m in range(8):
                d1.append(fw[0, m, :, cols] * e)
                d2.append(fw[1, m, :, cols] * (e - fw[2, m, :, cols]))
                ca.append(cacc[m, :, cols])
            for u in range(6):
                wu = jnp.broadcast_to(w_s[u : u + 1, cols], (8, 128))
                ga = None
                for m in range(8):
                    tm = g_ref[s, u, m, :, cols].astype(F32) * (d1[m] + wu * d2[m])
                    ca[m] = ca[m] + tm
                    ga = tm if ga is None else ga + tm
                v_s[u : u + 1, cols] = jnp.sum(ga, axis=0, keepdims=True)
            for m in range(8):
                cacc[m, :, cols] = ca[m]

    def scatter(s, v_s):
        qrow = q_ref[pl.ds(s, 1), :]
        v = v_s[...]
        v1 = v.astype(BF16).astype(F32)
        v2 = v - v1
        v12 = jnp.concatenate([v1, v2], axis=0).astype(BF16)
        hq = jnp.broadcast_to((qrow >> 8).astype(F32), (16, 512)).astype(BF16)
        a = [jnp.where(hq == jnp.full_like(hq, r), v12, jnp.zeros_like(v12)) for r in range(16)]
        gacc[...] += lax.dot_general(
            jnp.concatenate(a, axis=0), rows_like(io, 256, qrow & 255), (((1,), (1,)), ((), ())),
            preferred_element_type=F32,
        )

    look(0, xa, ya, ea, wa)

    def step(i, _):
        s = 8 * i
        look(s + 1, xb, yb, eb, wb)
        scatter(jnp.maximum(s - 1, 0), vb)
        contract(s, ea, wa, va)
        look(s + 2, xa, ya, ea, wa)
        scatter(s, va)
        contract(s + 1, eb, wb, vb)
        look(s + 3, xb, yb, eb, wb)
        scatter(s + 1, vb)
        contract(s + 2, ea, wa, va)
        look(s + 4, xa, ya, ea, wa)
        scatter(s + 2, va)
        contract(s + 3, eb, wb, vb)
        look(s + 5, xb, yb, eb, wb)
        scatter(s + 3, vb)
        contract(s + 4, ea, wa, va)
        look(s + 6, xa, ya, ea, wa)
        scatter(s + 4, va)
        contract(s + 5, eb, wb, vb)
        look(s + 7, xb, yb, eb, wb)
        scatter(s + 5, vb)
        contract(s + 6, ea, wa, va)
        look(jnp.minimum(s + 8, 15), xa, ya, ea, wa)
        scatter(s + 6, va)
        contract(s + 7, eb, wb, vb)
        return 0

    lax.fori_loop(0, 2, step, 0)
    scatter(15, vb)
    for m in range(8):
        c_ref[m : m + 1, :] = jnp.sum(cacc[m], axis=0, keepdims=True)
    gs = gacc[...].reshape(16, 2, 8, 256)
    gs = gs[:, 0] + gs[:, 1]
    for h in range(2):
        gen_ref[:, h] = gs[:, :, h * 128 : (h + 1) * 128]


VM = pl.BlockSpec(memory_space=pltpu.VMEM)
SM = pl.BlockSpec(memory_space=pltpu.SMEM)


def in_vmem(a):
    return pltpu.with_memory_space_constraint(a, pltpu.VMEM)


def in_hbm(a):
    return pltpu.with_memory_space_constraint(a, pltpu.HBM)


def phase(merge, par, own, oth, f, win, idx, q, g):
    scratch = [
        pltpu.VMEM((32, 2, 8, 512), BF16),
        pltpu.VMEM((512, 512), F32),
        pltpu.VMEM((512, 512), F32),
    ]
    own, oth, f, win, idx, q = map(in_vmem, (own, oth, f, win, idx, q))
    g = in_hbm(g)
    e = pl.pallas_call(
        own_kernel,
        out_shape=pltpu.VMEM((16, 8, 512), F32),
        in_specs=[SM, VM, VM],
        out_specs=VM,
        scratch_shapes=scratch,
        compiler_params=pltpu.CompilerParams(vmem_limit_bytes=12 << 20),
        name="own",
    )(par, own, idx)
    c, gen, pc = pl.pallas_call(
        functools.partial(main_kernel, merge),
        out_shape=(pltpu.VMEM((8, 512), F32), pltpu.VMEM((16, 2, 8, 128), F32), pltpu.VMEM((8, 128), F32)),
        in_specs=[SM] + [VM] * 7 + [pl.BlockSpec(memory_space=pltpu.HBM)],
        out_specs=(VM, VM, VM),
        scratch_shapes=[
            pltpu.VMEM((16, 6, 8, 8, 512), BF16),
            pltpu.VMEM((32, 2, 8, 512), BF16),
            pltpu.VMEM((16, 2, 8, 256), BF16),
            *([pltpu.VMEM((512, 512), F32), pltpu.VMEM((256, 512), F32)] * 2),
            *([pltpu.VMEM((8, 512), F32)] * 6),
            pltpu.VMEM((3, 8, 8, 512), F32),
            pltpu.VMEM((8, 8, 512), F32),
            pltpu.VMEM((256, 256), F32),
            pltpu.VMEM((256, 128), BF16),
            pltpu.SemaphoreType.DMA((16,)),
        ],
        compiler_params=pltpu.CompilerParams(vmem_limit_bytes=24 << 20),
        name="main",
    )(par, own, oth, in_vmem(e), f, win, idx, q, g)
    return c, gen.reshape(32, 8, 128), pc


def tiles(f):
    return f.reshape(8, 4, 128).transpose(1, 0, 2).reshape(32, 128)


def gather_all(send):
    own = lax.all_to_all(send, CHIPS, 0, 0, tiled=True)
    return own, lax.ppermute(own, "c", SWAP)


def on_device(f, p, g, idx, q, win):
    par = lax.axis_index("c").astype(I32)
    chip = (lax.axis_index("y") * 2 + lax.axis_index("zl")) * 4 + lax.axis_index("x")
    par1 = (chip.astype(I32) * 2 + par).reshape(1)
    f, p, idx, q, win = map(in_hbm, (f, p, idx, q, win))
    send, f, idx, q, win = pl.pallas_call(
        start_kernel,
        out_shape=(
            pltpu.VMEM((32, 40, 128), F32), pltpu.VMEM((8, 512), F32), pltpu.VMEM((16, 512), I32),
            pltpu.VMEM((16, 512), I32), pltpu.VMEM((8, 512), I32),
        ),
        in_specs=[SM] + [VM] * 5,
        out_specs=(VM,) * 5,
        compiler_params=pltpu.CompilerParams(vmem_limit_bytes=8 << 20),
        name="start",
    )(par1, f, p, idx, q, win)
    own, oth = gather_all(send)

    def reduce_gen(gen):
        got = lax.all_to_all(gen, CHIPS, 0, 0, tiled=True)
        got = jnp.sum(got, axis=0)
        return (got + lax.ppermute(got, "c", SWAP)) / 16.0

    def add_br(c):
        other = lax.ppermute(c, "br", SWAP)
        return c + other

    c1, gen1, pc = phase(True, par1, own, oth, f, win, idx, q, g)
    gen1 = reduce_gen(gen1)
    f2 = f + 0.1 * add_br(c1)
    p2 = pc + 0.1 * gen1
    chunk = jnp.concatenate([tiles(f2), p2], axis=0)
    own, oth = gather_all(jnp.broadcast_to(chunk[None], (32, 40, 128)))
    c2, gen2, _ = phase(False, par1, own, oth, f2, win, idx, q, g)
    gen2 = reduce_gen(gen2)
    gen2 = jnp.where(par == 0, gen2[:6, :64], gen2[:6, 64:])
    return add_br(c2), gen2


def solution(mesh):
    fine = Mesh(mesh.devices.reshape(4, 2, 4, 2, 2), ("y", "zl", "x", "c", "br"))
    ka = ("y", "zl", "x", "c")
    in_specs = (
        P(None, ka), P("br", ka), P(None, "br", None, None, ka), P(None, ka), P(None, ka), P(None, ka),
    )
    out_specs = (P(None, ka), P("br", ka))
    return jax.shard_map(on_device, mesh=fine, in_specs=in_specs, out_specs=out_specs, check_vma=False)
```

```python
import functools
import jax
import jax.numpy as jnp
from jax import lax
from jax.experimental import pallas as pl
from jax.experimental.pallas import tpu as pltpu
from jax.sharding import Mesh, PartitionSpec as P


F32 = jnp.float32
BF16 = jnp.bfloat16
I32 = jnp.int32
CHIPS = ("y", "zl", "x")
SWAP = [(0, 1), (1, 0)]


def split2(a):
    hi = a.astype(BF16)
    return hi, (a - hi.astype(F32)).astype(BF16)


def rows_are(sel, index):
    io = lax.broadcasted_iota(I32, (sel, index.shape[1]), 0)
    return jnp.where(io == index, 1.0, 0.0).astype(BF16)


def rows_like(io, sel, index):
    blocks = []
    for base in range(0, sel, 256):
        rel = jnp.broadcast_to((index - base).astype(F32), (16, index.shape[1])).astype(BF16)
        for b in range(16):
            row = jnp.concatenate([io[b * 16 : b * 16 + 16, :]] * (index.shape[1] // 128), axis=1)
            blocks.append(jnp.where(row == rel, jnp.ones_like(rel), jnp.zeros_like(rel)))
    return jnp.concatenate(blocks, axis=0)


def table_parts(tab_ref, t2):
    for kb in range(4):
        for part, val in enumerate(split2(tab_ref[:, kb * 8 : (kb + 1) * 8, :])):
            t2[:, part, :, kb * 128 : (kb + 1) * 128] = val


def pick(count, index, x):
    index = jnp.broadcast_to(index, (8, 512))
    hi = jnp.zeros((8, 512), F32)
    lo = jnp.zeros((8, 512), F32)
    for r in range(count):
        hit = index == r
        hi = jnp.where(hit, x[r * 16 : r * 16 + 8, :], hi)
        lo = jnp.where(hit, x[r * 16 + 8 : r * 16 + 16, :], lo)
    return hi + lo


def look_up(t2, x, row, parity, io=None):
    lo = jnp.where(((row >> 9) & 1) == parity, row & 511, -1)
    oh = rows_are(512, lo) if io is None else rows_like(io, 512, lo)
    x[...] = jnp.dot(t2.reshape(512, 512)[...], oh, preferred_element_type=F32)
    return pick(32, row >> 10, x)


def start_kernel(par_ref, f_ref, p_ref, idx_ref, q_ref, win_ref, send_ref, f_out, idx_out, q_out, win_out):
    p = p_ref[...]
    lane = lax.broadcasted_iota(I32, (6, 128), 1)
    p = jnp.where((lane >> 6) == (par_ref[0] & 1), jnp.concatenate([p, p], axis=1), 0.0)
    for kb in range(4):
        tile = f_ref[:, kb * 128 : (kb + 1) * 128]
        send_ref[:, kb * 8 : (kb + 1) * 8, :] = jnp.broadcast_to(tile[None], (32, 8, 128))
    p = jnp.concatenate([p, jnp.zeros((2, 128), F32)], axis=0)
    send_ref[:, 32:40, :] = jnp.broadcast_to(p[None], (32, 8, 128))
    f_out[...] = f_ref[...]
    idx_out[...] = idx_ref[...]
    q_out[...] = q_ref[...]
    win_out[...] = win_ref[...]


def own_kernel(par_ref, own_ref, idx_ref, e_ref, t2, xa, xb, io):
    io[...] = lax.broadcasted_iota(I32, (256, 128), 0).astype(F32).astype(BF16)
    par = par_ref[0] & 1
    table_parts(own_ref, t2)

    def step(i, _):
        for k, x in enumerate((xa, xb) * 8):
            s = i * 16 + k
            e_ref[s] = look_up(t2, x, idx_ref[pl.ds(s, 1), :], par, io)
        return 0

    lax.fori_loop(0, 1, step, 0)


def main_kernel(
    merge, par_ref, own_ref, oth_ref, e_ref, f_ref, win_ref, idx_ref, q_ref, g_hbm,
    c_ref, gen_ref, pc_ref, g_ref, t2, p2, xa, ya, xb, yb, ea, wa, va, eb, wb, vb, fw, cacc, gacc, io, sems,
):
    for s in range(16):
        pltpu.make_async_copy(g_hbm.at[s], g_ref.at[s], sems.at[s]).start()
    other = 1 - (par_ref[0] & 1)
    table_parts(oth_ref, t2)
    ph = own_ref[:, 32:40, :]
    if merge:
        ph = ph + oth_ref[:, 32:40, :]
    pc = own_ref[par_ref[0] >> 1, 32:40, :]
    if merge:
        pc = pc + oth_ref[par_ref[0] >> 1, 32:40, :]
    pc_ref[...] = pc
    ph = ph.reshape(16, 2, 8, 128)
    for h in range(2):
        for part, val in enumerate(split2(ph[:, h])):
            p2[:, part, :, h * 128 : (h + 1) * 128] = val
    for m in range(8):
        fm = jnp.broadcast_to(f_ref[m : m + 1, :], (8, 512))
        wm = jnp.broadcast_to(win_ref[m : m + 1, :].astype(F32), (8, 512))
        fw[0, m] = wm * (1.0 - fm)
        fw[1, m] = wm
        fw[2, m] = fm
    io[...] = lax.broadcasted_iota(I32, (256, 128), 0).astype(F32).astype(BF16)
    cacc[...] = jnp.zeros_like(cacc)
    gacc[...] = jnp.zeros_like(gacc)
    va[...] = jnp.zeros_like(va)
    vb[...] = jnp.zeros_like(vb)

    def look(s, x, y, e_s, w_s):
        qrow = q_ref[pl.ds(s, 1), :]
        y[...] = jnp.dot(
            p2.reshape(256, 256)[...], rows_like(io, 256, qrow & 255), preferred_element_type=F32
        )
        e_s[...] = look_up(t2, x, idx_ref[pl.ds(s, 1), :], other, io) + e_ref[s]
        w_s[...] = pick(16, qrow >> 8, y)

    def contract(s, e_s, w_s, v_s):
        pltpu.make_async_copy(g_hbm.at[s], g_ref.at[s], sems.at[s]).wait()
        for kb in range(4):
            cols = slice(kb * 128, (kb + 1) * 128)
            e = e_s[:, cols]
            d1, d2, ca = [], [], []
            for m in range(8):
                d1.append(fw[0, m, :, cols] * e)
                d2.append(fw[1, m, :, cols] * (e - fw[2, m, :, cols]))
                ca.append(cacc[m, :, cols])
            for u in range(6):
                wu = jnp.broadcast_to(w_s[u : u + 1, cols], (8, 128))
                ga = None
                for m in range(8):
                    tm = g_ref[s, u, m, :, cols].astype(F32) * (d1[m] + wu * d2[m])
                    ca[m] = ca[m] + tm
                    ga = tm if ga is None else ga + tm
                v_s[u : u + 1, cols] = jnp.sum(ga, axis=0, keepdims=True)
            for m in range(8):
                cacc[m, :, cols] = ca[m]

    def scatter(s, v_s):
        qrow = q_ref[pl.ds(s, 1), :]
        v = v_s[...]
        v1 = v.astype(BF16).astype(F32)
        v2 = v - v1
        v12 = jnp.concatenate([v1, v2], axis=0).astype(BF16)
        hq = jnp.broadcast_to((qrow >> 8).astype(F32), (16, 512)).astype(BF16)
        a = [jnp.where(hq == jnp.full_like(hq, r), v12, jnp.zeros_like(v12)) for r in range(16)]
        gacc[...] += lax.dot_general(
            jnp.concatenate(a, axis=0), rows_like(io, 256, qrow & 255), (((1,), (1,)), ((), ())),
            preferred_element_type=F32,
        )

    look(0, xa, ya, ea, wa)

    def step(i, _):
        s = 8 * i
        look(s + 1, xb, yb, eb, wb)
        scatter(jnp.maximum(s - 1, 0), vb)
        contract(s, ea, wa, va)
        look(s + 2, xa, ya, ea, wa)
        scatter(s, va)
        contract(s + 1, eb, wb, vb)
        look(s + 3, xb, yb, eb, wb)
        scatter(s + 1, vb)
        contract(s + 2, ea, wa, va)
        look(s + 4, xa, ya, ea, wa)
        scatter(s + 2, va)
        contract(s + 3, eb, wb, vb)
        look(s + 5, xb, yb, eb, wb)
        scatter(s + 3, vb)
        contract(s + 4, ea, wa, va)
        look(s + 6, xa, ya, ea, wa)
        scatter(s + 4, va)
        contract(s + 5, eb, wb, vb)
        look(s + 7, xb, yb, eb, wb)
        scatter(s + 5, vb)
        contract(s + 6, ea, wa, va)
        look(jnp.minimum(s + 8, 15), xa, ya, ea, wa)
        scatter(s + 6, va)
        contract(s + 7, eb, wb, vb)
        return 0

    lax.fori_loop(0, 2, step, 0)
    scatter(15, vb)
    for m in range(8):
        c_ref[m : m + 1, :] = jnp.sum(cacc[m], axis=0, keepdims=True)
    gs = gacc[...].reshape(16, 2, 8, 256)
    gs = gs[:, 0] + gs[:, 1]
    for h in range(2):
        gen_ref[:, h] = gs[:, :, h * 128 : (h + 1) * 128]


VM = pl.BlockSpec(memory_space=pltpu.VMEM)
SM = pl.BlockSpec(memory_space=pltpu.SMEM)


def in_vmem(a):
    return pltpu.with_memory_space_constraint(a, pltpu.VMEM)


def in_hbm(a):
    return pltpu.with_memory_space_constraint(a, pltpu.HBM)


def phase(merge, par, own, oth, f, win, idx, q, g):
    scratch = [
        pltpu.VMEM((32, 2, 8, 512), BF16),
        pltpu.VMEM((512, 512), F32),
        pltpu.VMEM((512, 512), F32),
        pltpu.VMEM((256, 128), BF16),
    ]
    own, oth, f, win, idx, q = map(in_vmem, (own, oth, f, win, idx, q))
    g = in_hbm(g)
    e = pl.pallas_call(
        own_kernel,
        out_shape=pltpu.VMEM((16, 8, 512), F32),
        in_specs=[SM, VM, VM],
        out_specs=VM,
        scratch_shapes=scratch,
        compiler_params=pltpu.CompilerParams(vmem_limit_bytes=12 << 20),
        name="own",
    )(par, own, idx)
    c, gen, pc = pl.pallas_call(
        functools.partial(main_kernel, merge),
        out_shape=(pltpu.VMEM((8, 512), F32), pltpu.VMEM((16, 2, 8, 128), F32), pltpu.VMEM((8, 128), F32)),
        in_specs=[SM] + [VM] * 7 + [pl.BlockSpec(memory_space=pltpu.HBM)],
        out_specs=(VM, VM, VM),
        scratch_shapes=[
            pltpu.VMEM((16, 6, 8, 8, 512), BF16),
            pltpu.VMEM((32, 2, 8, 512), BF16),
            pltpu.VMEM((16, 2, 8, 256), BF16),
            *([pltpu.VMEM((512, 512), F32), pltpu.VMEM((256, 512), F32)] * 2),
            *([pltpu.VMEM((8, 512), F32)] * 6),
            pltpu.VMEM((3, 8, 8, 512), F32),
            pltpu.VMEM((8, 8, 512), F32),
            pltpu.VMEM((256, 256), F32),
            pltpu.VMEM((256, 128), BF16),
            pltpu.SemaphoreType.DMA((16,)),
        ],
        compiler_params=pltpu.CompilerParams(vmem_limit_bytes=24 << 20),
        name="main",
    )(par, own, oth, in_vmem(e), f, win, idx, q, g)
    return c, gen.reshape(32, 8, 128), pc


def tiles(f):
    return f.reshape(8, 4, 128).transpose(1, 0, 2).reshape(32, 128)


def gather_all(send):
    own = lax.all_to_all(send, CHIPS, 0, 0, tiled=True)
    return own, lax.ppermute(own, "c", SWAP)


def on_device(f, p, g, idx, q, win):
    par = lax.axis_index("c").astype(I32)
    chip = (lax.axis_index("y") * 2 + lax.axis_index("zl")) * 4 + lax.axis_index("x")
    par1 = (chip.astype(I32) * 2 + par).reshape(1)
    f, p, idx, q, win = map(in_hbm, (f, p, idx, q, win))
    send, f, idx, q, win = pl.pallas_call(
        start_kernel,
        out_shape=(
            pltpu.VMEM((32, 40, 128), F32), pltpu.VMEM((8, 512), F32), pltpu.VMEM((16, 512), I32),
            pltpu.VMEM((16, 512), I32), pltpu.VMEM((8, 512), I32),
        ),
        in_specs=[SM] + [VM] * 5,
        out_specs=(VM,) * 5,
        compiler_params=pltpu.CompilerParams(vmem_limit_bytes=8 << 20),
        name="start",
    )(par1, f, p, idx, q, win)
    own, oth = gather_all(send)

    def reduce_gen(gen):
        got = lax.all_to_all(gen, CHIPS, 0, 0, tiled=True)
        got = jnp.sum(got, axis=0)
        return (got + lax.ppermute(got, "c", SWAP)) / 16.0

    def add_br(c):
        other = lax.ppermute(c, "br", SWAP)
        return c + other

    c1, gen1, pc = phase(True, par1, own, oth, f, win, idx, q, g)
    gen1 = reduce_gen(gen1)
    f2 = f + 0.1 * add_br(c1)
    p2 = pc + 0.1 * gen1
    chunk = jnp.concatenate([tiles(f2), p2], axis=0)
    own, oth = gather_all(jnp.broadcast_to(chunk[None], (32, 40, 128)))
    c2, gen2, _ = phase(False, par1, own, oth, f2, win, idx, q, g)
    gen2 = reduce_gen(gen2)
    gen2 = jnp.where(par == 0, gen2[:6, :64], gen2[:6, 64:])
    return add_br(c2), gen2


def solution(mesh):
    fine = Mesh(mesh.devices.reshape(4, 2, 4, 2, 2), ("y", "zl", "x", "c", "br"))
    ka = ("y", "zl", "x", "c")
    in_specs = (
        P(None, ka), P("br", ka), P(None, "br", None, None, ka), P(None, ka), P(None, ka), P(None, ka),
    )
    out_specs = (P(None, ka), P("br", ka))
    return jax.shard_map(on_device, mesh=fine, in_specs=in_specs, out_specs=out_specs, check_vma=False)
```
